768 devices in a mesh: section: 32 (over x_lo, y, core), dp: 24 (over z, x_hi).
Axes of the slice: x: 4 (x_hi: 2, x_lo: 2; x = x_hi * 2 + x_lo), y: 8, z: 12, core: 2. Of those that a mesh axis runs over, the one named last changes fastest.
Arguments:
- queries: bfloat16 [24576, 6144], P('section', 'dp'), may hold values from -6 to 6
- key_input: bfloat16 [24576, 6144], P('section', 'dp'), may hold values from -6 to 6
- values_in: bfloat16 [24576, 6144], P('section', 'dp'), may hold values from -6 to 6
- cotangent: bfloat16 [24576, 6144], P('section', 'dp'), may hold values from -6 to 6
- norm_gain: bfloat16 [6144], P('dp'), may hold values from 0.099609375 to 1.8984375
- decay_log: float32 [48], P('dp'), as said below
- doc_starts: int32 [24576], P('section'), may hold values 0 or 1
Outputs:
- grad_query: bfloat16 [24576, 6144], P('section', 'dp')
- grad_key: bfloat16 [24576, 6144], P('section', 'dp')
- grad_value: bfloat16 [24576, 6144], P('section', 'dp')
- grad_gain: float32 [6144], P('dp')
The draws below stay inside these ranges and needn't reach their ends.
Inputs may be any that keep to these rules, and one draw needn't show every extreme that they name: `doc_starts`: 1 marks a token that begins a new document: no state passes into it from earlier tokens. `decay_log`: negative for every head.
All inputs are finite; a program needn't handle non-finite values. No bound on the sum of `doc_starts` on one device may be relied on, other than what follows from the above.
Results may differ from the reference program's by a relative error of at most 0.001.
Values sent between devices are 32-bit elements; how exact they have to be, the bound alone decides.
A program may use at most 64 MiB of HBM per device.

```python
import math
import jax
import jax.numpy as jnp
from jax import lax

H = 48
DH = 128
LEN = 24576


def draw_decay_log(key, part):
    first = jax.random.fold_in(key, 0)
    spread = jax.random.uniform(first, (H,), jnp.float32)
    lowest = math.log(1.0 / (64.0 * LEN))
    highest = math.log(1.0 / 30.0)
    rate = jnp.exp(lowest + spread * (highest - lowest))
    return -rate


def set_ends(drawn, own_key, least, top_value):
    extent = drawn.shape
    spot = [jax.random.randint(jax.random.fold_in(own_key, axis), (), 0, extent[axis]) for axis in range(len(extent))]
    drawn = drawn.at[tuple(spot)].set(least)
    longest = extent.index(max(extent))
    spot[longest] = (spot[longest] + 1) % extent[longest]
    return drawn.at[tuple(spot)].set(top_value)


def levels(own_key, extent, cuts, smallest, top_value):
    def one(axis_at, parts):
        heights = jax.random.uniform(jax.random.fold_in(jax.random.fold_in(own_key, 6), axis_at), (parts,), jnp.float32, smallest / len(cuts), top_value / len(cuts))
        return jnp.repeat(jnp.exp(heights), extent[axis_at] // parts).reshape((-1,) + (1,) * (len(extent) - axis_at - 1))

    loudness = one(*cuts[0])
    for cut in cuts[1:]:
        loudness = loudness * one(*cut)
    return loudness


def centred(own_key, extent, scale, bound, cuts=(), kind=jnp.bfloat16):
    gain = levels(own_key, extent, cuts, -0.22, 0.18) if cuts else 1.0
    entries = jax.random.normal(own_key, extent, jnp.float32) * scale * gain
    return jnp.minimum(jnp.maximum(entries, -bound), bound).astype(kind)


def setup_inputs(seed: int = 0) -> dict:
    keys = jax.random.split(jax.random.key(seed), 8)
    queries = centred(keys[0], (LEN, H * DH), 1.0, 6.0, ((0, 32), (1, 24)))
    key_input = centred(keys[1], (LEN, H * DH), 1.0, 6.0, ((0, 32), (1, 24)))
    values_in = centred(keys[2], (LEN, H * DH), 1.0, 6.0, ((0, 32), (1, 24)))
    cotangent = centred(keys[3], (LEN, H * DH), 1.0, 6.0, ((0, 32), (1, 24)))
    norm_gain = jnp.clip(1.0 + 0.18 * jax.random.normal(keys[4], (H * DH,), jnp.float32), 0.099609375, 1.8984375).astype(jnp.bfloat16)
    decay_log = draw_decay_log(jax.random.fold_in(keys[7], 71), 0)
    doc_starts = set_ends((jax.random.randint(keys[6], (LEN,), 0, LEN) < 4).astype(jnp.int32), jax.random.fold_in(keys[6], 1), 0, 1)
    return dict(queries=queries, key_input=key_input, values_in=values_in, cotangent=cotangent, norm_gain=norm_gain, decay_log=decay_log, doc_starts=doc_starts)


epsilon = 1e-05

def to_heads(array, heads):
    rows, width = array.shape
    return array.reshape(rows, heads, width // heads).transpose(1, 0, 2)

def to_rows(array):
    heads, rows, part = array.shape
    return array.transpose(1, 0, 2).reshape(rows, heads * part)

def block_factors(doc_starts, decay_log):
    count = doc_starts.shape[0]
    segment = jnp.cumsum(doc_starts).astype(jnp.int32)
    position = jnp.arange(1, count + 1).astype(jnp.float32)
    offset = position[:, None] - position[None, :]
    keep = (offset >= 0.0) & (segment[:, None] == segment[None, :])
    masks = jnp.where(keep[None], jnp.exp(decay_log[:, None, None] * jnp.maximum(offset, 0.0)[None]), 0.0)
    prefix = jnp.where((segment == 0)[None], jnp.exp(decay_log[:, None] * position[None]), 0.0)
    suffix = jnp.where((segment == segment[-1])[None], jnp.exp(decay_log[:, None] * (count - position)[None]), 0.0)
    total = jnp.where(segment[-1] == 0, jnp.exp(decay_log * count), 0.0)
    return (masks, prefix, suffix, total)

def matmul(left, right):
    return jnp.matmul(left, right, precision=lax.Precision.HIGHEST)

def reference(queries, key_input, values_in, cotangent, norm_gain, decay_log, doc_starts):
    query_heads = to_heads(queries, H).astype(jnp.float32)
    key_heads = to_heads(key_input, H).astype(jnp.float32)
    value_heads = to_heads(values_in, H).astype(jnp.float32)
    upstream = to_heads(cotangent, H).astype(jnp.float32)
    gain_heads = norm_gain.astype(jnp.float32).reshape(H, 1, DH)
    block = math.gcd(LEN, 256)
    blocks = LEN // block
    starts_blocks = doc_starts.reshape(blocks, block)

    def forward_states(query, keyed, value, rate):
        rates = rate[None]

        def forward(state, xs):
            qb, kb, vb, sb = xs
            masks, prefix, suffix, total = block_factors(sb, rates)
            masks, prefix, suffix, total = (masks[0], prefix[0], suffix[0], total[0])
            scores = masks * matmul(qb, kb.T)
            outputs = matmul(scores, vb) + prefix[:, None] * matmul(qb, state)
            state_next = total * state + matmul((suffix[:, None] * kb).T, vb)
            return (state_next, (outputs, state))
        start = jnp.zeros((DH, DH), jnp.float32)
        _, (outputs, states_in) = lax.scan(forward, start, (query, keyed, value, starts_blocks))
        return (outputs, states_in)

    def head_forward(items):
        query, keyed, value, rate = items
        outputs, _ = forward_states(query.reshape(blocks, block, DH), keyed.reshape(blocks, block, DH), value.reshape(blocks, block, DH), rate)
        return outputs.reshape(LEN, DH)
    outputs = lax.map(head_forward, (query_heads, key_heads, value_heads, decay_log))
    features = H * DH
    square_total = lax.optimization_barrier(jnp.sum(outputs * outputs, axis=(0, 2)))
    scale_rows = lax.rsqrt(square_total / features + epsilon)
    normed = outputs * scale_rows[None, :, None]
    grad_norm = upstream * gain_heads
    mixed = lax.optimization_barrier(jnp.sum(grad_norm * normed, axis=(0, 2))) / features
    grad_out = scale_rows[None, :, None] * (grad_norm - normed * mixed[None, :, None])
    grad_gain = lax.optimization_barrier(jnp.sum(upstream * normed, axis=1)).reshape(H * DH) / math.sqrt(LEN)

    def head_backward(items):
        query, keyed, value, grad, rate = items
        query = query.reshape(blocks, block, DH)
        keyed = keyed.reshape(blocks, block, DH)
        value = value.reshape(blocks, block, DH)
        grad = grad.reshape(blocks, block, DH)
        rates = rate[None]
        _, states_in = forward_states(query, keyed, value, rate)

        def backward(carry, xs):
            qb, kb, vb, gb, sb, state = xs
            masks, prefix, suffix, total = block_factors(sb, rates)
            masks, prefix, suffix, total = (masks[0], prefix[0], suffix[0], total[0])
            scores = masks * matmul(qb, kb.T)
            grad_scores = masks * matmul(gb, vb.T)
            dq = matmul(grad_scores, kb) + prefix[:, None] * matmul(gb, state.T)
            dk = matmul(grad_scores.T, qb) + suffix[:, None] * matmul(vb, carry.T)
            dv = matmul(scores.T, gb) + suffix[:, None] * matmul(kb, carry)
            carry_next = total * carry + matmul((prefix[:, None] * qb).T, gb)
            return (carry_next, (dq, dk, dv))
        start = jnp.zeros((DH, DH), jnp.float32)
        _, (dq, dk, dv) = lax.scan(backward, start, (query, keyed, value, grad, starts_blocks, states_in), reverse=True)
        return (dq.reshape(LEN, DH), dk.reshape(LEN, DH), dv.reshape(LEN, DH))
    dq, dk, dv = lax.map(head_backward, (query_heads, key_heads, value_heads, grad_out, decay_log))
    return (to_rows(dq).astype(jnp.bfloat16), to_rows(dk).astype(jnp.bfloat16), to_rows(dv).astype(jnp.bfloat16), grad_gain)
```

```python
import functools
import math

import jax
import jax.numpy as jnp
from jax import lax
from jax.experimental import pallas as pl
from jax.experimental.pallas import tpu as pltpu
from jax.sharding import PartitionSpec as P

epsilon = 1e-05
MESH = pl.DeviceIdType.MESH
f32 = jnp.float32
bf16 = jnp.bfloat16


def split(x):
    hi = x.astype(bf16)
    return hi, (x - hi.astype(f32)).astype(bf16)


def nn(a, b):
    return lax.dot_general(a, b, (((1,), (0,)), ((), ())), preferred_element_type=f32)


def nt(a, b):
    return lax.dot_general(a, b, (((1,), (1,)), ((), ())), preferred_element_type=f32)


def tn(a, b):
    return lax.dot_general(a, b, (((0,), (0,)), ((), ())), preferred_element_type=f32)


def wide(*parts):
    return jnp.concatenate(parts, axis=1)


def column(row):
    return jnp.transpose(jnp.broadcast_to(row, (128, row.shape[1])))


def kernel(
    sections, columns, rows, block,
    q_ref, k_ref, v_ref, g_ref, gain_ref, decay_ref, doc_ref,
    gq_ref, gk_ref, gv_ref, gg_ref,
    flag_out, flag_in,
    f_out, f_in, p_out, state,
    b_out, b_in, c_out, carry,
    gain_out, gain_in,
    pair_out, pair_in, line_out, line_in,
    pre, suf, mask, s_hi, s_lo, o, d_hi, d_lo,
    send_sem, recv_sem,
):
    me = lax.axis_index("section")
    dp = lax.axis_index("dp")
    tiers = columns // 2
    x_at = dp % 2
    z_at = dp // 2
    half = sections // 2
    depth = 256 // sections
    features = 256 * columns
    blocks = rows // block

    def to_section(source, target, which, peer):
        return pltpu.make_async_remote_copy(
            src_ref=source, dst_ref=target, send_sem=send_sem.at[which],
            recv_sem=recv_sem.at[which], device_id={"section": peer}, device_id_type=MESH,
        )

    def to_column(source, target, which, peer):
        return pltpu.make_async_remote_copy(
            src_ref=source, dst_ref=target, send_sem=send_sem.at[which],
            recv_sem=recv_sem.at[which], device_id={"dp": peer}, device_id_type=MESH,
        )

    def spread(source_of, target, which):
        def one(step, _):
            peer = (me + step) % sections
            to_section(source_of(peer), target.at[me], which, peer).start()
            return 0

        lax.fori_loop(1, sections, one, 0)

    def all_but_one(buffer, which):
        part = buffer.at[pl.ds(0, sections - 1)]
        return to_section(part, part, which, (me + 1) % sections)

    barrier = pltpu.get_barrier_semaphore()

    def greet(step, _):
        pl.semaphore_signal(
            barrier, inc=1, device_id={"section": (me + step) % sections}, device_id_type=MESH
        )
        return 0

    def greet_line(step, _):
        pl.semaphore_signal(
            barrier, inc=1, device_id={"dp": ((z_at + step) % tiers) * 2 + x_at},
            device_id_type=MESH,
        )
        return 0

    lax.fori_loop(1, sections, greet, 0)
    other = z_at * 2 + (1 - x_at)
    pl.semaphore_signal(barrier, inc=1, device_id={"dp": other}, device_id_type=MESH)
    lax.fori_loop(1, tiers, greet_line, 0)

    docs = jnp.broadcast_to(doc_ref[...].astype(f32), (8, rows)).astype(bf16)
    upper = (
        lax.broadcasted_iota(jnp.int32, (128, 128), 0)
        <= lax.broadcasted_iota(jnp.int32, (128, 128), 1)
    ).astype(f32).astype(bf16)
    run = jnp.zeros((8, 1), f32)
    parts = []
    for at in range(rows // 128):
        part = nn(docs[:, at * 128 : (at + 1) * 128], upper) + run
        run = part[:, 127:128]
        parts.append(part)
    seg_row = wide(*parts)[0:1]
    last = run[0:1]
    seg = column(seg_row)
    position = lax.broadcasted_iota(jnp.int32, (rows, 128), 0).astype(f32) + 1.0

    def head_slice(h):
        return pl.ds(pl.multiple_of(h * 128, 128), 128)

    def local_states(h, _):
        decay = decay_ref[h]
        suffix = jnp.where(seg == last, jnp.exp(decay * (rows - position)), 0.0)
        prefix = jnp.where(seg == 0.0, jnp.exp(decay * position), 0.0)
        suf[h] = suffix
        pre[h] = prefix
        hi, lo = split(suffix * k_ref[:, head_slice(h)].astype(f32))
        both = tn(wide(hi, lo), v_ref[:, head_slice(h)])
        f_out[pl.ds(h * half, half)] = (both[0:128] + both[128:256]).reshape(half, depth, 128)
        return 0

    lax.fori_loop(0, 2, local_states, 0)
    flag = jnp.broadcast_to(jnp.where(last == 0.0, 1.0, 0.0), (1, 128))
    flag_out[...] = flag
    flag_in[me] = flag
    f_in[me] = f_out[me]

    pl.semaphore_wait(barrier, sections + tiers - 1)
    spread(lambda peer: f_out.at[peer], f_in, 0)
    spread(lambda peer: flag_out, flag_in, 1)

    def pairs(h, body):
        for at in range(blocks):
            for past in range(at + 1):
                body(h, at, past)

    def forward_pair(h, at, past):
        ti, si = pl.ds(at * block, block), pl.ds(past * block, block)
        offset = (
            lax.broadcasted_iota(jnp.int32, (block, block), 0)
            - lax.broadcasted_iota(jnp.int32, (block, block), 1)
            + (at - past) * block
        )
        here = seg[at * block : (at + 1) * block]
        keep = wide(here, here) == seg_row[:, past * block : (past + 1) * block]
        if at == past:
            keep = keep & (offset >= 0)
        weights = jnp.where(
            keep, jnp.exp(decay_ref[h] * jnp.maximum(offset, 0).astype(f32)), 0.0
        )
        mask[h, ti, si] = weights
        hi, lo = split(weights * nt(q_ref[ti, head_slice(h)], k_ref[si, head_slice(h)]))
        s_hi[h, ti, si] = hi
        s_lo[h, ti, si] = lo
        values = v_ref[si, head_slice(h)]
        term = nn(hi, values) + nn(lo, values)
        if past == 0:
            o[ti, head_slice(h)] = term
        else:
            o[ti, head_slice(h)] += term

    def forward_head(h, _):
        pairs(h, forward_pair)
        return 0

    lax.fori_loop(0, 2, forward_head, 0)

    def factors():
        rate = jnp.where(me < half, decay_ref[0], decay_ref[1])
        return jnp.exp(jnp.full((depth, 128), rate * rows, f32))

    all_but_one(f_in, 0).wait_recv()
    all_but_one(flag_in, 1).wait_recv()
    total = factors()
    held = jnp.zeros((depth, 128), f32)
    for at in range(sections):
        p_out[at] = held
        held = total * flag_in[at] * held + f_in[at]
    spread(lambda peer: p_out.at[peer], state, 2)
    state[me] = p_out[me]
    all_but_one(state, 2).wait_recv()

    def state_of(buffer, h):
        return split(buffer[pl.ds(h * half, half)].reshape(128, 128))

    def finish_outputs(h, _):
        hi, lo = state_of(state, h)
        both = nn(q_ref[:, head_slice(h)], wide(hi, lo))
        o[:, head_slice(h)] += pre[h] * (both[:, 0:128] + both[:, 128:256])
        return 0

    lax.fori_loop(0, 2, finish_outputs, 0)
    outputs = o[...]
    upstream = g_ref[...].astype(f32)
    grad_norm = upstream * gain_ref[...].astype(f32)
    squares = outputs * outputs
    mixes = grad_norm * outputs
    pair_out[0:1] = jnp.sum(jnp.transpose(squares[:, 0:128] + squares[:, 128:256]), 0, keepdims=True)
    pair_out[1:2] = jnp.sum(jnp.transpose(mixes[:, 0:128] + mixes[:, 128:256]), 0, keepdims=True)
    swap = to_column(pair_out, pair_in, 3, other)
    swap.start()
    swap.wait_recv()
    line = pair_out[...] + pair_in[...]
    line_out[...] = line
    line_in[z_at] = line

    def one_tier(step, _):
        peer = ((z_at + step) % tiers) * 2 + x_at
        to_column(line_out, line_in.at[z_at], 4, peer).start()
        return 0

    lax.fori_loop(1, tiers, one_tier, 0)
    tier_part = line_in.at[pl.ds(0, tiers - 1)]
    tier_wait = to_column(tier_part, tier_part, 4, other)
    tier_wait.wait_recv()
    sums = line_in[0]
    for at in range(1, tiers):
        sums = sums + line_in[at]
    scale = lax.rsqrt(sums[0:1] / features + epsilon)
    mixed = scale * sums[1:2] / features
    scale = column(scale)
    mixed = column(mixed)
    scale = wide(scale, scale)
    normed = outputs * scale
    grad_out = scale * (grad_norm - normed * wide(mixed, mixed))
    hi, lo = split(grad_out)
    d_hi[...] = hi
    d_lo[...] = lo
    gains = jnp.sum(upstream * normed, 0, keepdims=True)
    gain_out[0:1] = gains[:, 0:128]
    gain_out[1:2] = gains[:, 128:256]

    def backward_states(h, _):
        hi, lo = split(pre[h] * q_ref[:, head_slice(h)].astype(f32))
        four = tn(wide(hi, lo), wide(d_hi[:, head_slice(h)], d_lo[:, head_slice(h)]))
        top = four[0:128] + four[128:256]
        b_out[pl.ds(h * half, half)] = (top[:, 0:128] + top[:, 128:256]).reshape(half, depth, 128)
        return 0

    lax.fori_loop(0, 2, backward_states, 0)
    b_in[me] = b_out[me]
    gain_in[me] = gain_out[...]
    spread(lambda peer: b_out.at[peer], b_in, 5)
    spread(lambda peer: gain_out, gain_in, 6)

    def start_query(h, _):
        hi, lo = state_of(state, h)
        stack = jnp.concatenate([wide(hi, hi), wide(lo, lo)], axis=0)
        both = nt(wide(d_hi[:, head_slice(h)], d_lo[:, head_slice(h)]), stack)
        gq_ref[:, head_slice(h)] = pre[h] * (both[:, 0:128] + both[:, 128:256])
        return 0

    lax.fori_loop(0, 2, start_query, 0)

    all_but_one(b_in, 5).wait_recv()
    held = jnp.zeros((depth, 128), f32)
    for at in reversed(range(sections)):
        c_out[at] = held
        held = total * flag_in[at] * held + b_in[at]
    spread(lambda peer: c_out.at[peer], carry, 7)
    carry[me] = c_out[me]

    def backward_pair(h, at, past):
        ti, si = pl.ds(at * block, block), pl.ds(past * block, block)
        grads = wide(d_hi[ti, head_slice(h)], d_lo[ti, head_slice(h)])
        values = v_ref[si, head_slice(h)]
        hi, lo = split(mask[h, ti, si] * nt(grads, wide(values, values)))
        keys = k_ref[si, head_slice(h)]
        queries = q_ref[ti, head_slice(h)]
        gq_ref[ti, head_slice(h)] += nn(hi, keys) + nn(lo, keys)
        key_term = tn(hi, queries) + tn(lo, queries)
        both = tn(s_hi[h, ti, si], grads) + tn(s_lo[h, ti, si], grads)
        value_term = both[:, 0:128] + both[:, 128:256]
        if at == past:
            gk_ref[si, head_slice(h)] = key_term
            gv_ref[si, head_slice(h)] = value_term
        else:
            gk_ref[si, head_slice(h)] += key_term
            gv_ref[si, head_slice(h)] += value_term

    def backward_head(h, _):
        pairs(h, backward_pair)
        return 0

    lax.fori_loop(0, 2, backward_head, 0)
    all_but_one(gain_in, 6).wait_recv()
    gains = gain_in[0]
    for at in range(1, sections):
        gains = gains + gain_in[at]
    gg_ref[...] = gains / math.sqrt(rows * sections)
    all_but_one(carry, 7).wait_recv()

    def finish(h, _):
        hi, lo = state_of(carry, h)
        both = nt(v_ref[:, head_slice(h)], jnp.concatenate([hi, lo], axis=0))
        gk_ref[:, head_slice(h)] += suf[h] * (both[:, 0:128] + both[:, 128:256])
        both = nn(k_ref[:, head_slice(h)], wide(hi, lo))
        gv_ref[:, head_slice(h)] += suf[h] * (both[:, 0:128] + both[:, 128:256])
        return 0

    lax.fori_loop(0, 2, finish, 0)
    all_but_one(f_in, 0).wait_send()
    all_but_one(flag_in, 1).wait_send()
    all_but_one(state, 2).wait_send()
    swap.wait_send()
    tier_wait.wait_send()
    all_but_one(b_in, 5).wait_send()
    all_but_one(gain_in, 6).wait_send()
    all_but_one(carry, 7).wait_send()


def shards(queries, key_input, values_in, cotangent, norm_gain, decay_log, doc_starts):
    rows, width = queries.shape
    sections = lax.axis_size("section")
    columns = lax.axis_size("dp")
    depth = width // sections
    tiers = columns // 2
    vmem = pl.BlockSpec(memory_space=pltpu.VMEM)
    pieces = pltpu.VMEM((sections, depth, 128), f32)
    outs = pl.pallas_call(
        functools.partial(kernel, sections, columns, rows, 256),
        out_shape=[jax.ShapeDtypeStruct((rows, width), f32)] * 3
        + [jax.ShapeDtypeStruct((2, 128), f32)],
        in_specs=[vmem] * 5 + [pl.BlockSpec(memory_space=pltpu.SMEM), vmem],
        out_specs=[vmem] * 4,
        scratch_shapes=[
            pltpu.VMEM((1, 128), f32), pltpu.VMEM((sections, 1, 128), f32),
            pieces, pieces, pieces, pieces,
            pieces, pieces, pieces, pieces,
            pltpu.VMEM((2, 128), f32), pltpu.VMEM((sections, 2, 128), f32),
            pltpu.VMEM((2, rows), f32), pltpu.VMEM((2, rows), f32),
            pltpu.VMEM((2, rows), f32), pltpu.VMEM((tiers, 2, rows), f32),
            pltpu.VMEM((2, rows, 128), f32), pltpu.VMEM((2, rows, 128), f32),
            pltpu.VMEM((2, rows, rows), f32),
            pltpu.VMEM((2, rows, rows), bf16), pltpu.VMEM((2, rows, rows), bf16),
            pltpu.VMEM((rows, width), f32),
            pltpu.VMEM((rows, width), bf16), pltpu.VMEM((rows, width), bf16),
            pltpu.SemaphoreType.DMA((8,)), pltpu.SemaphoreType.DMA((8,)),
        ],
        compiler_params=pltpu.CompilerParams(
            collective_id=0, has_side_effects=True, vmem_limit_bytes=48 * 1024 * 1024
        ),
        name="layer_grads",
    )(
        queries, key_input, values_in, cotangent, norm_gain.reshape(1, width), decay_log,
        doc_starts.reshape(1, rows),
    )
    return (
        outs[0].astype(bf16), outs[1].astype(bf16), outs[2].astype(bf16), outs[3].reshape(width),
    )


def solution(mesh):
    in_specs = (
        P("section", "dp"),
        P("section", "dp"),
        P("section", "dp"),
        P("section", "dp"),
        P("dp"),
        P("dp"),
        P("section"),
    )
    out_specs = (P("section", "dp"), P("section", "dp"), P("section", "dp"), P("dp"))
    return jax.shard_map(shards, mesh=mesh, in_specs=in_specs, out_specs=out_specs, check_vma=False)
```

```python
import functools
import math

import jax
import jax.numpy as jnp
from jax import lax
from jax.experimental import pallas as pl
from jax.experimental.pallas import tpu as pltpu
from jax.sharding import PartitionSpec as P

epsilon = 1e-05
MESH = pl.DeviceIdType.MESH
f32 = jnp.float32
bf16 = jnp.bfloat16


def split(x):
    hi = x.astype(bf16)
    return hi, (x - hi.astype(f32)).astype(bf16)


def nn(a, b):
    return lax.dot_general(a, b, (((1,), (0,)), ((), ())), preferred_element_type=f32)


def nt(a, b):
    return lax.dot_general(a, b, (((1,), (1,)), ((), ())), preferred_element_type=f32)


def tn(a, b):
    return lax.dot_general(a, b, (((0,), (0,)), ((), ())), preferred_element_type=f32)


def wide(*parts):
    return jnp.concatenate(parts, axis=1)


def column(row):
    return jnp.transpose(jnp.broadcast_to(row, (128, row.shape[1])))


def kernel(
    sections, columns, rows, block,
    q_hbm, k_hbm, v_hbm, g_hbm, gain_hbm, decay_ref, doc_hbm,
    gq_ref, gk_ref, gv_ref, gg_ref,
    q_ref, k_ref, v_ref, g_ref, gain_ref, doc_ref, local_sem,
    f_out, f_in, p_out, state,
    b_out, b_in, c_out, carry,
    gain_out, gain_in,
    pair_out, pair_in, line_out, line_in,
    pre, suf, mask, s_hi, s_lo, o, d_hi, d_lo,
    send_sem, recv_sem,
):
    me = lax.axis_index("section")
    dp = lax.axis_index("dp")
    tiers = columns // 2
    x_at = dp % 2
    z_at = dp // 2
    half = sections // 2
    depth = 256 // sections
    features = 256 * columns
    blocks = rows // block
    pending = []

    def to_section(source, target, which, peer):
        return pltpu.make_async_remote_copy(
            src_ref=source, dst_ref=target, send_sem=send_sem.at[which],
            recv_sem=recv_sem.at[which], device_id={"section": peer}, device_id_type=MESH,
        )

    def to_column(source, target, which, peer):
        return pltpu.make_async_remote_copy(
            src_ref=source, dst_ref=target, send_sem=send_sem.at[which],
            recv_sem=recv_sem.at[which], device_id={"dp": peer}, device_id_type=MESH,
        )

    tall = sections // 4
    hops = sorted(range(tall), key=lambda y: -min(y, tall - y))
    steps = [
        (x, y, c) for y in hops for x in (1, 0) for c in (1, 0) if (x, y, c) != (0, 0, 0)
    ]

    def peer_at(x, y, c):
        return (
            ((me // (2 * tall) + x) % 2) * (2 * tall)
            + ((me // 2 + y) % tall) * 2
            + (me + c) % 2
        )

    def spread(source_of, target, which):
        for step in steps:
            peer = peer_at(*step)
            to_section(source_of(peer), target.at[me], which, peer).start()

    def all_but_one(buffer, which):
        part = buffer.at[pl.ds(0, sections - 1)]
        return to_section(part, part, which, (me + 1) % sections)

    loads = []
    for at, (source, target) in enumerate(
        [
            (doc_hbm, doc_ref), (k_hbm, k_ref), (v_hbm, v_ref),
            (q_hbm, q_ref), (g_hbm, g_ref), (gain_hbm, gain_ref),
        ]
    ):
        load = pltpu.make_async_copy(source, target, local_sem.at[at])
        load.start()
        loads.append(load)

    barrier = pltpu.get_barrier_semaphore()

    def greet(step, _):
        pl.semaphore_signal(
            barrier, inc=1, device_id={"section": (me + step) % sections}, device_id_type=MESH
        )
        return 0

    def greet_line(step, _):
        pl.semaphore_signal(
            barrier, inc=1, device_id={"dp": ((z_at + step) % tiers) * 2 + x_at},
            device_id_type=MESH,
        )
        return 0

    lax.fori_loop(1, sections, greet, 0)
    other = z_at * 2 + (1 - x_at)
    pl.semaphore_signal(barrier, inc=1, device_id={"dp": other}, device_id_type=MESH)
    lax.fori_loop(1, tiers, greet_line, 0)

    loads[0].wait()
    upper = (
        lax.broadcasted_iota(jnp.int32, (128, 128), 0)
        <= lax.broadcasted_iota(jnp.int32, (128, 128), 1)
    ).astype(f32).astype(bf16)
    run = jnp.zeros((8, 1), f32)
    parts = []
    for at in range(rows // 128):
        docs = doc_ref[pl.ds(at * 128, 128)].astype(f32)
        part = nn(jnp.broadcast_to(docs[None, :], (8, 128)).astype(bf16), upper) + run
        run = part[:, 127:128]
        parts.append(part)
    seg_row = wide(*parts)[0:1]
    last = run[0:1]
    seg = column(seg_row)
    position = lax.broadcasted_iota(jnp.int32, (rows, 128), 0).astype(f32) + 1.0

    def head_slice(h):
        return pl.ds(pl.multiple_of(h * 128, 128), 128)

    def local_states(h, _):
        decay = decay_ref[h]
        suffix = jnp.where(seg == last, jnp.exp(decay * (rows - position)), 0.0)
        prefix = jnp.where(seg == 0.0, jnp.exp(decay * position), 0.0)
        suf[h] = suffix
        pre[h] = prefix
        hi, lo = split(suffix * k_ref[:, head_slice(h)].astype(f32))
        both = tn(wide(hi, lo), v_ref[:, head_slice(h)])
        f_out[pl.ds(h * half, half), 0:depth] = (both[0:128] + both[128:256]).reshape(half, depth, 128)
        return 0

    f_out[:, depth : depth + 1] = jnp.broadcast_to(
        jnp.where(last == 0.0, 1.0, 0.0)[None], (sections, 1, 128)
    )
    loads[1].wait()
    loads[2].wait()
    lax.fori_loop(0, 2, local_states, 0)
    f_in[me] = f_out[me]

    pl.semaphore_wait(barrier, sections + tiers - 1)
    spread(lambda peer: f_out.at[peer], f_in, 0)
    pending.append(all_but_one(f_in, 0))

    def pairs(h, body):
        for at in range(blocks):
            for past in range(at + 1):
                body(h, at, past)

    def forward_pair(h, at, past):
        ti, si = pl.ds(at * block, block), pl.ds(past * block, block)
        offset = (
            lax.broadcasted_iota(jnp.int32, (block, block), 0)
            - lax.broadcasted_iota(jnp.int32, (block, block), 1)
            + (at - past) * block
        )
        here = seg[at * block : (at + 1) * block]
        keep = wide(here, here) == seg_row[:, past * block : (past + 1) * block]
        if at == past:
            keep = keep & (offset >= 0)
        weights = jnp.where(
            keep, jnp.exp(decay_ref[h] * jnp.maximum(offset, 0).astype(f32)), 0.0
        )
        mask[h, ti, si] = weights
        hi, lo = split(weights * nt(q_ref[ti, head_slice(h)], k_ref[si, head_slice(h)]))
        s_hi[h, ti, si] = hi
        s_lo[h, ti, si] = lo
        values = v_ref[si, head_slice(h)]
        term = nn(hi, values) + nn(lo, values)
        if past == 0:
            o[ti, head_slice(h)] = term
        else:
            o[ti, head_slice(h)] += term

    def forward_head(h, _):
        pairs(h, forward_pair)
        return 0

    loads[3].wait()
    lax.fori_loop(0, 1, forward_head, 0)

    def factors():
        rate = jnp.where(me < half, decay_ref[0], decay_ref[1])
        return jnp.exp(jnp.full((depth, 128), rate * rows, f32))

    all_but_one(f_in, 0).wait_recv()
    total = factors()
    held = jnp.zeros((depth, 128), f32)
    for at in range(sections):
        p_out[at] = held
        held = total * f_in[at, depth : depth + 1] * held + f_in[at, 0:depth]
    spread(lambda peer: p_out.at[peer], state, 2)
    pending.append(all_but_one(state, 2))
    state[me] = p_out[me]
    lax.fori_loop(1, 2, forward_head, 0)
    all_but_one(state, 2).wait_recv()

    def state_of(buffer, h):
        return split(buffer[pl.ds(h * half, half)].reshape(128, 128))

    def finish_outputs(h, _):
        hi, lo = state_of(state, h)
        both = nn(q_ref[:, head_slice(h)], wide(hi, lo))
        o[:, head_slice(h)] += pre[h] * (both[:, 0:128] + both[:, 128:256])
        return 0

    lax.fori_loop(0, 2, finish_outputs, 0)
    loads[4].wait()
    loads[5].wait()
    outputs = o[...]
    upstream = g_ref[...].astype(f32)
    grad_norm = upstream * gain_ref[...].astype(f32)[None, :]
    squares = outputs * outputs
    mixes = grad_norm * outputs
    pair_out[0:1] = jnp.sum(jnp.transpose(squares[:, 0:128] + squares[:, 128:256]), 0, keepdims=True)
    pair_out[1:2] = jnp.sum(jnp.transpose(mixes[:, 0:128] + mixes[:, 128:256]), 0, keepdims=True)
    swap = to_column(pair_out, pair_in, 3, other)
    swap.start()
    pending.append(swap)
    swap.wait_recv()
    line = pair_out[...] + pair_in[...]
    line_out[...] = line
    line_in[z_at] = line

    def one_tier(step, _):
        peer = ((z_at + step) % tiers) * 2 + x_at
        to_column(line_out, line_in.at[z_at], 4, peer).start()
        return 0

    lax.fori_loop(1, tiers, one_tier, 0)
    tier_part = line_in.at[pl.ds(0, tiers - 1)]
    tier_wait = to_column(tier_part, tier_part, 4, other)
    pending.append(tier_wait)
    tier_wait.wait_recv()
    sums = line_in[0]
    for at in range(1, tiers):
        sums = sums + line_in[at]
    scale = lax.rsqrt(sums[0:1] / features + epsilon)
    mixed = scale * sums[1:2] / features
    scale = column(scale)
    mixed = column(mixed)
    scale = wide(scale, scale)
    normed = outputs * scale
    grad_out = scale * (grad_norm - normed * wide(mixed, mixed))
    hi, lo = split(grad_out)
    d_hi[...] = hi
    d_lo[...] = lo
    gains = jnp.sum(upstream * normed, 0, keepdims=True)
    gain_out[0:1] = gains[:, 0:128]
    gain_out[1:2] = gains[:, 128:256]

    def backward_states(h, _):
        hi, lo = split(pre[h] * q_ref[:, head_slice(h)].astype(f32))
        four = tn(wide(hi, lo), wide(d_hi[:, head_slice(h)], d_lo[:, head_slice(h)]))
        top = four[0:128] + four[128:256]
        b_out[pl.ds(h * half, half)] = (top[:, 0:128] + top[:, 128:256]).reshape(half, depth, 128)
        return 0

    lax.fori_loop(0, 2, backward_states, 0)
    b_in[me] = b_out[me]
    gain_in[me] = gain_out[...]
    spread(lambda peer: b_out.at[peer], b_in, 5)
    pending.append(all_but_one(b_in, 5))

    def start_query(h, _):
        hi, lo = state_of(state, h)
        stack = jnp.concatenate([wide(hi, hi), wide(lo, lo)], axis=0)
        both = nt(wide(d_hi[:, head_slice(h)], d_lo[:, head_slice(h)]), stack)
        gq_ref[:, head_slice(h)] = pre[h] * (both[:, 0:128] + both[:, 128:256])
        return 0

    lax.fori_loop(0, 2, start_query, 0)

    def backward_pair(h, at, past):
        ti, si = pl.ds(at * block, block), pl.ds(past * block, block)
        grads = wide(d_hi[ti, head_slice(h)], d_lo[ti, head_slice(h)])
        values = v_ref[si, head_slice(h)]
        hi, lo = split(mask[h, ti, si] * nt(grads, wide(values, values)))
        keys = k_ref[si, head_slice(h)]
        queries = q_ref[ti, head_slice(h)]
        gq_ref[ti, head_slice(h)] += nn(hi, keys) + nn(lo, keys)
        key_term = tn(hi, queries) + tn(lo, queries)
        both = tn(s_hi[h, ti, si], grads) + tn(s_lo[h, ti, si], grads)
        value_term = both[:, 0:128] + both[:, 128:256]
        if at == past:
            gk_ref[si, head_slice(h)] = key_term
            gv_ref[si, head_slice(h)] = value_term
        else:
            gk_ref[si, head_slice(h)] += key_term
            gv_ref[si, head_slice(h)] += value_term

    def backward_head(h, _):
        pairs(h, backward_pair)
        return 0

    lax.fori_loop(0, 1, backward_head, 0)
    all_but_one(b_in, 5).wait_recv()
    held = jnp.zeros((depth, 128), f32)
    for at in reversed(range(sections)):
        c_out[at] = held
        held = total * f_in[at, depth : depth + 1] * held + b_in[at]
    spread(lambda peer: c_out.at[peer], carry, 7)
    pending.append(all_but_one(carry, 7))
    spread(lambda peer: gain_out, gain_in, 6)
    pending.append(all_but_one(gain_in, 6))
    carry[me] = c_out[me]
    lax.fori_loop(1, 2, backward_head, 0)
    all_but_one(carry, 7).wait_recv()

    def finish(h, _):
        hi, lo = state_of(carry, h)
        both = nt(v_ref[:, head_slice(h)], jnp.concatenate([hi, lo], axis=0))
        gk_ref[:, head_slice(h)] += suf[h] * (both[:, 0:128] + both[:, 128:256])
        both = nn(k_ref[:, head_slice(h)], wide(hi, lo))
        gv_ref[:, head_slice(h)] += suf[h] * (both[:, 0:128] + both[:, 128:256])
        return 0

    lax.fori_loop(0, 2, finish, 0)
    all_but_one(gain_in, 6).wait_recv()
    gains = gain_in[0]
    for at in range(1, sections):
        gains = gains + gain_in[at]
    gg_ref[...] = gains / math.sqrt(rows * sections)
    for copy in pending:
        copy.wait_send()


def store_kernel(gq_ref, gk_ref, gv_ref, gg_ref, gq_hbm, gk_hbm, gv_hbm, gain_ref, cast, sems):
    copies = []
    for at, (source, target) in enumerate(
        [(gq_ref, gq_hbm), (gk_ref, gk_hbm), (gv_ref, gv_hbm)]
    ):
        cast[at] = source[...].astype(bf16)
        copy = pltpu.make_async_copy(cast.at[at], target, sems.at[at])
        copy.start()
        copies.append(copy)
    gain_ref[pl.ds(0, 128)] = gg_ref[0]
    gain_ref[pl.ds(128, 128)] = gg_ref[1]
    for copy in copies:
        copy.wait()


def shards(queries, key_input, values_in, cotangent, norm_gain, decay_log, doc_starts):
    rows, width = queries.shape
    sections = lax.axis_size("section")
    columns = lax.axis_size("dp")
    depth = width // sections
    tiers = columns // 2
    vmem = pl.BlockSpec(memory_space=pltpu.VMEM)
    hbm = pl.BlockSpec(memory_space=pltpu.HBM)
    smem = pl.BlockSpec(memory_space=pltpu.SMEM)
    pieces = pltpu.VMEM((sections, depth, 128), f32)
    flagged = pltpu.VMEM((sections, depth + 1, 128), f32)
    tokens = pltpu.VMEM((rows, width), bf16)
    outs = pl.pallas_call(
        functools.partial(kernel, sections, columns, rows, 256),
        out_shape=[jax.ShapeDtypeStruct((rows, width), f32)] * 3
        + [jax.ShapeDtypeStruct((2, 128), f32)],
        in_specs=[hbm] * 5 + [smem, hbm],
        out_specs=[vmem] * 4,
        scratch_shapes=[
            tokens, tokens, tokens, tokens,
            pltpu.VMEM((width,), bf16), pltpu.VMEM((rows,), jnp.int32),
            pltpu.SemaphoreType.DMA((6,)),
            flagged, flagged, pieces, pieces,
            pieces, pieces, pieces, pieces,
            pltpu.VMEM((2, 128), f32), pltpu.VMEM((sections, 2, 128), f32),
            pltpu.VMEM((2, rows), f32), pltpu.VMEM((2, rows), f32),
            pltpu.VMEM((2, rows), f32), pltpu.VMEM((tiers, 2, rows), f32),
            pltpu.VMEM((2, rows, 128), f32), pltpu.VMEM((2, rows, 128), f32),
            pltpu.VMEM((2, rows, rows), f32),
            pltpu.VMEM((2, rows, rows), bf16), pltpu.VMEM((2, rows, rows), bf16),
            pltpu.VMEM((rows, width), f32),
            tokens, tokens,
            pltpu.SemaphoreType.DMA((8,)), pltpu.SemaphoreType.DMA((8,)),
        ],
        compiler_params=pltpu.CompilerParams(
            collective_id=0, has_side_effects=True, vmem_limit_bytes=48 * 1024 * 1024
        ),
        name="layer_grads",
    )(
        *(
            pltpu.with_memory_space_constraint(x, pltpu.HBM)
            for x in (queries, key_input, values_in, cotangent, norm_gain)
        ),
        decay_log,
        pltpu.with_memory_space_constraint(doc_starts, pltpu.HBM),
    )
    return tuple(
        pl.pallas_call(
            store_kernel,
            out_shape=[jax.ShapeDtypeStruct((rows, width), bf16)] * 3
            + [jax.ShapeDtypeStruct((width,), f32)],
            in_specs=[vmem] * 4,
            out_specs=[hbm] * 3 + [vmem],
            scratch_shapes=[
                pltpu.VMEM((3, rows, width), bf16), pltpu.SemaphoreType.DMA((3,)),
            ],
            compiler_params=pltpu.CompilerParams(vmem_limit_bytes=8 * 1024 * 1024),
            name="store_grads",
        )(*outs)
    )


def solution(mesh):
    in_specs = (
        P("section", "dp"),
        P("section", "dp"),
        P("section", "dp"),
        P("section", "dp"),
        P("dp"),
        P("dp"),
        P("section"),
    )
    out_specs = (P("section", "dp"), P("section", "dp"), P("section", "dp"), P("dp"))
    return jax.shard_map(shards, mesh=mesh, in_specs=in_specs, out_specs=out_specs, check_vma=False)
```

```python
import functools
import math

import jax
import jax.numpy as jnp
from jax import lax
from jax.experimental import pallas as pl
from jax.experimental.pallas import tpu as pltpu
from jax.sharding import PartitionSpec as P

epsilon = 1e-05
MESH = pl.DeviceIdType.MESH
f32 = jnp.float32
bf16 = jnp.bfloat16


def split(x):
    hi = x.astype(bf16)
    return hi, (x - hi.astype(f32)).astype(bf16)


def nn(a, b):
    return lax.dot_general(a, b, (((1,), (0,)), ((), ())), preferred_element_type=f32)


def nt(a, b):
    return lax.dot_general(a, b, (((1,), (1,)), ((), ())), preferred_element_type=f32)


def tn(a, b):
    return lax.dot_general(a, b, (((0,), (0,)), ((), ())), preferred_element_type=f32)


def wide(*parts):
    return jnp.concatenate(parts, axis=1)


def column(row):
    return jnp.transpose(jnp.broadcast_to(row, (128, row.shape[1])))


def kernel(
    sections, columns, rows, block,
    q_hbm, k_hbm, v_hbm, g_hbm, gain_hbm, decay_hbm, doc_hbm,
    gq_out, gk_out, gv_out, gg_ref,
    gq_ref, gk_ref, gv_ref, decay_ref,
    q_ref, k_ref, v_ref, g_ref, gain_ref, doc_ref, local_sem,
    f_out, f_in, p_out, state,
    b_out, b_in, c_out, carry,
    gain_out, gain_in,
    pair_out, pair_in, line_out, line_in,
    pre, suf, mask, s_hi, s_lo, o, d_hi, d_lo,
    send_sem, recv_sem,
):
    me = lax.axis_index("section")
    dp = lax.axis_index("dp")
    tiers = columns // 2
    x_at = dp % 2
    z_at = dp // 2
    half = sections // 2
    depth = 256 // sections
    features = 256 * columns
    blocks = rows // block
    pending = []

    def to_section(source, target, which, peer):
        return pltpu.make_async_remote_copy(
            src_ref=source, dst_ref=target, send_sem=send_sem.at[which],
            recv_sem=recv_sem.at[which], device_id={"section": peer}, device_id_type=MESH,
        )

    def to_column(source, target, which, peer):
        return pltpu.make_async_remote_copy(
            src_ref=source, dst_ref=target, send_sem=send_sem.at[which],
            recv_sem=recv_sem.at[which], device_id={"dp": peer}, device_id_type=MESH,
        )

    tall = sections // 4
    hops = sorted(range(tall), key=lambda y: -min(y, tall - y))
    steps = [
        (x, y, c) for y in hops for x in (1, 0) for c in (1, 0) if (x, y, c) != (0, 0, 0)
    ]

    def peer_at(x, y, c):
        return (
            ((me // (2 * tall) + x) % 2) * (2 * tall)
            + ((me // 2 + y) % tall) * 2
            + (me + c) % 2
        )

    def spread(source_of, target, which):
        for step in steps:
            peer = peer_at(*step)
            to_section(source_of(peer), target.at[me], which, peer).start()

    def all_but_one(buffer, which):
        part = buffer.at[pl.ds(0, sections - 1)]
        return to_section(part, part, which, (me + 1) % sections)

    barrier = pltpu.get_barrier_semaphore()
    other = z_at * 2 + (1 - x_at)
    line_hops = sorted(range(1, tiers), key=lambda z: -min(z, tiers - z))

    def line_peer(hop):
        return ((z_at + hop) % tiers) * 2 + x_at

    def greet(peer):
        pl.semaphore_signal(barrier, inc=1, device_id=peer, device_id_type=MESH)

    for hop in line_hops:
        greet({"dp": line_peer(hop)})
    for step in steps:
        greet({"section": peer_at(*step)})
    greet({"dp": other})

    loads = []
    for at, (source, target) in enumerate(
        [
            (doc_hbm, doc_ref), (k_hbm, k_ref), (v_hbm, v_ref),
            (q_hbm, q_ref), (g_hbm, g_ref), (gain_hbm, gain_ref), (decay_hbm, decay_ref),
        ]
    ):
        load = pltpu.make_async_copy(source, target, local_sem.at[at])
        load.start()
        loads.append(load)

    loads[0].wait()
    upper = (
        lax.broadcasted_iota(jnp.int32, (128, 128), 0)
        <= lax.broadcasted_iota(jnp.int32, (128, 128), 1)
    ).astype(f32).astype(bf16)
    run = jnp.zeros((8, 1), f32)
    parts = []
    for at in range(rows // 128):
        docs = doc_ref[pl.ds(at * 128, 128)].astype(f32)
        part = nn(jnp.broadcast_to(docs[None, :], (8, 128)).astype(bf16), upper) + run
        run = part[:, 127:128]
        parts.append(part)
    seg_row = wide(*parts)[0:1]
    last = run[0:1]
    seg = column(seg_row)
    position = lax.broadcasted_iota(jnp.int32, (rows, 128), 0).astype(f32) + 1.0

    def head_slice(h):
        return pl.ds(pl.multiple_of(h * 128, 128), 128)

    def local_states(h, _):
        decay = decay_ref[h]
        suffix = jnp.where(seg == last, jnp.exp(decay * (rows - position)), 0.0)
        prefix = jnp.where(seg == 0.0, jnp.exp(decay * position), 0.0)
        suf[h] = suffix
        pre[h] = prefix
        hi, lo = split(suffix * k_ref[:, head_slice(h)].astype(f32))
        both = tn(wide(hi, lo), v_ref[:, head_slice(h)])
        f_out[pl.ds(h * half, half), 0:depth] = (both[0:128] + both[128:256]).reshape(half, depth, 128)
        return 0

    f_out[:, depth : depth + 1] = jnp.broadcast_to(
        jnp.where(last == 0.0, 1.0, 0.0)[None], (sections, 1, 128)
    )
    loads[1].wait()
    loads[2].wait()
    loads[6].wait()
    lax.fori_loop(0, 2, local_states, 0)
    f_in[me] = f_out[me]

    pl.semaphore_wait(barrier, sections + tiers - 1)
    spread(lambda peer: f_out.at[peer], f_in, 0)
    pending.append(all_but_one(f_in, 0))

    loads[3].wait()

    def pairs(h, body):
        for at in range(blocks):
            for past in range(at + 1):
                body(h, at, past)

    def forward_pair(h, at, past):
        ti, si = pl.ds(at * block, block), pl.ds(past * block, block)
        offset = (
            lax.broadcasted_iota(jnp.int32, (block, block), 0)
            - lax.broadcasted_iota(jnp.int32, (block, block), 1)
            + (at - past) * block
        )
        here = seg[at * block : (at + 1) * block]
        keep = wide(here, here) == seg_row[:, past * block : (past + 1) * block]
        if at == past:
            keep = keep & (offset >= 0)
        weights = jnp.where(
            keep, jnp.exp(decay_ref[h] * jnp.maximum(offset, 0).astype(f32)), 0.0
        )
        mask[h, ti, si] = weights
        hi, lo = split(weights * nt(q_ref[ti, head_slice(h)], k_ref[si, head_slice(h)]))
        s_hi[h, ti, si] = hi
        s_lo[h, ti, si] = lo
        values = v_ref[si, head_slice(h)]
        term = nn(hi, values) + nn(lo, values)
        if past == 0:
            o[ti, head_slice(h)] = term
        else:
            o[ti, head_slice(h)] += term

    rate = jnp.where(me < half, decay_ref[0], decay_ref[1])
    total = jnp.exp(jnp.full((depth, 128), rate * rows, f32))
    f_all, state_all = all_but_one(f_in, 0), all_but_one(state, 2)

    def forward_head(h, _):
        pairs(h, forward_pair)

        @pl.when(h == 0)
        def _():
            f_all.wait_recv()
            held = jnp.zeros((depth, 128), f32)
            for at in range(sections):
                p_out[at] = held
                held = total * f_in[at, depth : depth + 1] * held + f_in[at, 0:depth]
            spread(lambda peer: p_out.at[peer], state, 2)

        return 0

    lax.fori_loop(0, 2, forward_head, 0)
    pending.append(state_all)
    state[me] = p_out[me]
    state_all.wait_recv()

    def state_of(buffer, h):
        return split(buffer[pl.ds(h * half, half)].reshape(128, 128))

    def finish_outputs(h, _):
        hi, lo = state_of(state, h)
        both = nn(q_ref[:, head_slice(h)], wide(hi, lo))
        o[:, head_slice(h)] += pre[h] * (both[:, 0:128] + both[:, 128:256])
        return 0

    lax.fori_loop(0, 2, finish_outputs, 0)
    loads[4].wait()
    loads[5].wait()
    outputs = o[...]
    upstream = g_ref[...].astype(f32)
    grad_norm = upstream * gain_ref[...].astype(f32)[None, :]
    squares = outputs * outputs
    mixes = grad_norm * outputs
    pair_out[0:1] = jnp.sum(jnp.transpose(squares[:, 0:128] + squares[:, 128:256]), 0, keepdims=True)
    pair_out[1:2] = jnp.sum(jnp.transpose(mixes[:, 0:128] + mixes[:, 128:256]), 0, keepdims=True)
    swap = to_column(pair_out, pair_in, 3, other)
    swap.start()
    pending.append(swap)
    swap.wait_recv()
    line = pair_out[...] + pair_in[...]
    line_out[...] = line
    line_in[z_at] = line

    for hop in line_hops:
        to_column(line_out, line_in.at[z_at], 4, line_peer(hop)).start()
    tier_part = line_in.at[pl.ds(0, tiers - 1)]
    tier_wait = to_column(tier_part, tier_part, 4, other)
    pending.append(tier_wait)
    tier_wait.wait_recv()
    sums = line_in[0]
    for at in range(1, tiers):
        sums = sums + line_in[at]
    scale = lax.rsqrt(sums[0:1] / features + epsilon)
    mixed = scale * sums[1:2] / features
    scale = column(scale)
    mixed = column(mixed)
    scale = wide(scale, scale)
    normed = outputs * scale
    grad_out = scale * (grad_norm - normed * wide(mixed, mixed))
    hi, lo = split(grad_out)
    d_hi[...] = hi
    d_lo[...] = lo
    gains = jnp.sum(upstream * normed, 0, keepdims=True)
    gain_out[0:1] = gains[:, 0:128]
    gain_out[1:2] = gains[:, 128:256]

    def backward_states(h, _):
        hi, lo = split(pre[h] * q_ref[:, head_slice(h)].astype(f32))
        four = tn(wide(hi, lo), wide(d_hi[:, head_slice(h)], d_lo[:, head_slice(h)]))
        top = four[0:128] + four[128:256]
        b_out[pl.ds(h * half, half)] = (top[:, 0:128] + top[:, 128:256]).reshape(half, depth, 128)
        return 0

    lax.fori_loop(0, 2, backward_states, 0)
    b_in[me] = b_out[me]
    gain_in[me] = gain_out[...]
    spread(lambda peer: b_out.at[peer], b_in, 5)
    pending.append(all_but_one(b_in, 5))

    def start_query(h, _):
        hi, lo = state_of(state, h)
        stack = jnp.concatenate([wide(hi, hi), wide(lo, lo)], axis=0)
        both = nt(wide(d_hi[:, head_slice(h)], d_lo[:, head_slice(h)]), stack)
        gq_ref[:, head_slice(h)] = pre[h] * (both[:, 0:128] + both[:, 128:256])
        return 0

    lax.fori_loop(0, 2, start_query, 0)

    def backward_pair(h, at, past):
        ti, si = pl.ds(at * block, block), pl.ds(past * block, block)
        grads = wide(d_hi[ti, head_slice(h)], d_lo[ti, head_slice(h)])
        values = v_ref[si, head_slice(h)]
        hi, lo = split(mask[h, ti, si] * nt(grads, wide(values, values)))
        keys = k_ref[si, head_slice(h)]
        queries = q_ref[ti, head_slice(h)]
        gq_ref[ti, head_slice(h)] += nn(hi, keys) + nn(lo, keys)
        key_term = tn(hi, queries) + tn(lo, queries)
        both = tn(s_hi[h, ti, si], grads) + tn(s_lo[h, ti, si], grads)
        value_term = both[:, 0:128] + both[:, 128:256]
        if at == past:
            gk_ref[si, head_slice(h)] = key_term
            gv_ref[si, head_slice(h)] = value_term
        else:
            gk_ref[si, head_slice(h)] += key_term
            gv_ref[si, head_slice(h)] += value_term

    b_all, carry_all = all_but_one(b_in, 5), all_but_one(carry, 7)

    def backward_head(h, _):
        pairs(h, backward_pair)
        gq_out[:, head_slice(h)] = gq_ref[:, head_slice(h)].astype(bf16)

        @pl.when(h == 0)
        def _():
            b_all.wait_recv()
            held = jnp.zeros((depth, 128), f32)
            for at in reversed(range(sections)):
                c_out[at] = held
                held = total * f_in[at, depth : depth + 1] * held + b_in[at]
            spread(lambda peer: c_out.at[peer], carry, 7)
            spread(lambda peer: gain_out, gain_in, 6)

        return 0

    lax.fori_loop(0, 2, backward_head, 0)
    pending.append(carry_all)
    pending.append(all_but_one(gain_in, 6))
    carry[me] = c_out[me]
    carry_all.wait_recv()

    def finish(h, _):
        hi, lo = state_of(carry, h)
        both = nt(v_ref[:, head_slice(h)], jnp.concatenate([hi, lo], axis=0))
        grads = gk_ref[:, head_slice(h)] + suf[h] * (both[:, 0:128] + both[:, 128:256])
        gk_out[:, head_slice(h)] = grads.astype(bf16)
        both = nn(k_ref[:, head_slice(h)], wide(hi, lo))
        grads = gv_ref[:, head_slice(h)] + suf[h] * (both[:, 0:128] + both[:, 128:256])
        gv_out[:, head_slice(h)] = grads.astype(bf16)
        return 0

    lax.fori_loop(0, 2, finish, 0)
    all_but_one(gain_in, 6).wait_recv()
    gains = gain_in[0]
    for at in range(1, sections):
        gains = gains + gain_in[at]
    gg_ref[...] = gains / math.sqrt(rows * sections)
    for copy in pending:
        copy.wait_send()


def store_kernel(gq_ref, gk_ref, gv_ref, gg_ref, gq_hbm, gk_hbm, gv_hbm, gain_ref, sems):
    copies = []
    for at, (source, target) in enumerate(
        [(gq_ref, gq_hbm), (gk_ref, gk_hbm), (gv_ref, gv_hbm)]
    ):
        copy = pltpu.make_async_copy(source, target, sems.at[at])
        copy.start()
        copies.append(copy)
    gain_ref[pl.ds(0, 128)] = gg_ref[0]
    gain_ref[pl.ds(128, 128)] = gg_ref[1]
    for copy in copies:
        copy.wait()


def shards(queries, key_input, values_in, cotangent, norm_gain, decay_log, doc_starts):
    rows, width = queries.shape
    sections = lax.axis_size("section")
    columns = lax.axis_size("dp")
    depth = width // sections
    tiers = columns // 2
    vmem = pl.BlockSpec(memory_space=pltpu.VMEM)
    hbm = pl.BlockSpec(memory_space=pltpu.HBM)
    sums = pltpu.VMEM((rows, width), f32)
    pieces = pltpu.VMEM((sections, depth, 128), f32)
    flagged = pltpu.VMEM((sections, depth + 1, 128), f32)
    tokens = pltpu.VMEM((rows, width), bf16)
    outs = pl.pallas_call(
        functools.partial(kernel, sections, columns, rows, 256),
        out_shape=[jax.ShapeDtypeStruct((rows, width), bf16)] * 3
        + [jax.ShapeDtypeStruct((2, 128), f32)],
        in_specs=[hbm] * 7,
        out_specs=[vmem] * 4,
        scratch_shapes=[
            sums, sums, sums, pltpu.SMEM((2,), f32),
            tokens, tokens, tokens, tokens,
            pltpu.VMEM((width,), bf16), pltpu.VMEM((rows,), jnp.int32),
            pltpu.SemaphoreType.DMA((7,)),
            flagged, flagged, pieces, pieces,
            pieces, pieces, pieces, pieces,
            pltpu.VMEM((2, 128), f32), pltpu.VMEM((sections, 2, 128), f32),
            pltpu.VMEM((2, rows), f32), pltpu.VMEM((2, rows), f32),
            pltpu.VMEM((2, rows), f32), pltpu.VMEM((tiers, 2, rows), f32),
            pltpu.VMEM((2, rows, 128), f32), pltpu.VMEM((2, rows, 128), f32),
            pltpu.VMEM((2, rows, rows), f32),
            pltpu.VMEM((2, rows, rows), bf16), pltpu.VMEM((2, rows, rows), bf16),
            pltpu.VMEM((rows, width), f32),
            tokens, tokens,
            pltpu.SemaphoreType.DMA((8,)), pltpu.SemaphoreType.DMA((8,)),
        ],
        compiler_params=pltpu.CompilerParams(
            collective_id=0, has_side_effects=True, vmem_limit_bytes=48 * 1024 * 1024
        ),
        name="layer_grads",
    )(
        *(
            pltpu.with_memory_space_constraint(x, pltpu.HBM)
            for x in (
                queries, key_input, values_in, cotangent, norm_gain, decay_log, doc_starts,
            )
        )
    )
    return tuple(
        pl.pallas_call(
            store_kernel,
            out_shape=[jax.ShapeDtypeStruct((rows, width), bf16)] * 3
            + [jax.ShapeDtypeStruct((width,), f32)],
            in_specs=[vmem] * 4,
            out_specs=[hbm] * 3 + [vmem],
            scratch_shapes=[pltpu.SemaphoreType.DMA((3,))],
            compiler_params=pltpu.CompilerParams(vmem_limit_bytes=8 * 1024 * 1024),
            name="store_grads",
        )(*outs)
    )


def solution(mesh):
    in_specs = (
        P("section", "dp"),
        P("section", "dp"),
        P("section", "dp"),
        P("section", "dp"),
        P("dp"),
        P("dp"),
        P("section"),
    )
    out_specs = (P("section", "dp"), P("section", "dp"), P("section", "dp"), P("dp"))
    return jax.shard_map(shards, mesh=mesh, in_specs=in_specs, out_specs=out_specs, check_vma=False)
```

```python
import functools
import math

import jax
import jax.numpy as jnp
from jax import lax
from jax.experimental import pallas as pl
from jax.experimental.pallas import tpu as pltpu
from jax.sharding import PartitionSpec as P

epsilon = 1e-05
MESH = pl.DeviceIdType.MESH
f32 = jnp.float32
bf16 = jnp.bfloat16


def split(x):
    hi = x.astype(bf16)
    return hi, (x - hi.astype(f32)).astype(bf16)


def nn(a, b):
    return lax.dot_general(a, b, (((1,), (0,)), ((), ())), preferred_element_type=f32)


def nt(a, b):
    return lax.dot_general(a, b, (((1,), (1,)), ((), ())), preferred_element_type=f32)


def tn(a, b):
    return lax.dot_general(a, b, (((0,), (0,)), ((), ())), preferred_element_type=f32)


def wide(*parts):
    return jnp.concatenate(parts, axis=1)


def column(row):
    return jnp.transpose(jnp.broadcast_to(row, (128, row.shape[1])))


def kernel(
    sections, columns, rows, block,
    q_hbm, k_hbm, v_hbm, g_hbm, gain_hbm, decay_hbm, doc_hbm,
    gq_out, gk_ref, gv_ref, gg_ref, carry_out, suf, k_ref, v_ref,
    gq_ref, decay_ref,
    q_ref, g_ref, gain_ref, doc_ref, local_sem,
    f_out, f_in, p_out, state,
    b_out, b_in, c_out, carry,
    gain_out, gain_in,
    pair_out, near_in, line_out, far_in, turned,
    pre, mask, s_hi, s_lo, o, d_hi, d_lo,
    send_sem, recv_sem,
):
    me = lax.axis_index("section")
    dp = lax.axis_index("dp")
    tiers = columns // 2
    x_at = dp % 2
    z_at = dp // 2
    half = sections // 2
    depth = 256 // sections
    features = 256 * columns
    blocks = rows // block
    pending = []

    def to_section(source, target, which, peer):
        return pltpu.make_async_remote_copy(
            src_ref=source, dst_ref=target, send_sem=send_sem.at[which],
            recv_sem=recv_sem.at[which], device_id={"section": peer}, device_id_type=MESH,
        )

    def to_column(source, target, which, peer):
        return pltpu.make_async_remote_copy(
            src_ref=source, dst_ref=target, send_sem=send_sem.at[which],
            recv_sem=recv_sem.at[which], device_id={"dp": peer}, device_id_type=MESH,
        )

    tall = sections // 4
    hops = sorted(range(tall), key=lambda y: -min(y, tall - y))
    steps = [
        (x, y, c) for y in hops for x in (1, 0) for c in (1, 0) if (x, y, c) != (0, 0, 0)
    ]

    def peer_at(x, y, c):
        return (
            ((me // (2 * tall) + x) % 2) * (2 * tall)
            + ((me // 2 + y) % tall) * 2
            + (me + c) % 2
        )

    def spread(source_of, target, which):
        for step in steps:
            peer = peer_at(*step)
            to_section(source_of(peer), target.at[me], which, peer).start()

    def all_but_one(buffer, which):
        part = buffer.at[pl.ds(0, sections - 1)]
        return to_section(part, part, which, (me + 1) % sections)

    barrier = pltpu.get_barrier_semaphore()
    reach = 3 if tiers % 3 == 0 else 1
    near = [(z, 1) for z in (1, tiers - 1)[: reach - 1]] + [(0, 1)]
    near += [(z, 0) for z in (1, tiers - 1)[: reach - 1]]
    far = sorted(range(reach, tiers, reach), key=lambda z: -min(z, tiers - z))

    def line_peer(z, x):
        return ((z_at + z) % tiers) * 2 + (x_at + x) % 2

    def greet(peer):
        pl.semaphore_signal(barrier, inc=1, device_id=peer, device_id_type=MESH)

    for z in far:
        greet({"dp": line_peer(z, 0)})
    for step in steps:
        greet({"section": peer_at(*step)})
    for z, x in near:
        greet({"dp": line_peer(z, x)})

    loads = []
    for at, (source, target) in enumerate(
        [
            (doc_hbm, doc_ref), (k_hbm, k_ref), (v_hbm, v_ref),
            (q_hbm, q_ref), (g_hbm, g_ref), (gain_hbm, gain_ref), (decay_hbm, decay_ref),
        ]
    ):
        load = pltpu.make_async_copy(source, target, local_sem.at[at])
        load.start()
        loads.append(load)

    loads[0].wait()
    upper = (
        lax.broadcasted_iota(jnp.int32, (128, 128), 0)
        <= lax.broadcasted_iota(jnp.int32, (128, 128), 1)
    ).astype(f32).astype(bf16)
    run = jnp.zeros((8, 1), f32)
    parts = []
    for at in range(rows // 128):
        docs = doc_ref[pl.ds(at * 128, 128)].astype(f32)
        part = nn(jnp.broadcast_to(docs[None, :], (8, 128)).astype(bf16), upper) + run
        run = part[:, 127:128]
        parts.append(part)
    seg_row = wide(*parts)[0:1]
    last = run[0:1]
    seg = column(seg_row)
    position = lax.broadcasted_iota(jnp.int32, (rows, 128), 0).astype(f32) + 1.0

    def head_slice(h):
        return pl.ds(pl.multiple_of(h * 128, 128), 128)

    def local_states(h, _):
        decay = decay_ref[h]
        suffix = jnp.where(seg == last, jnp.exp(decay * (rows - position)), 0.0)
        prefix = jnp.where(seg == 0.0, jnp.exp(decay * position), 0.0)
        suf[h] = suffix
        pre[h] = prefix
        hi, lo = split(suffix * k_ref[:, head_slice(h)].astype(f32))
        both = tn(wide(hi, lo), v_ref[:, head_slice(h)])
        f_out[pl.ds(h * half, half), 0:depth] = (both[0:128] + both[128:256]).reshape(half, depth, 128)
        return 0

    f_out[:, depth : depth + 1] = jnp.broadcast_to(
        jnp.where(last == 0.0, 1.0, 0.0)[None], (sections, 1, 128)
    )
    loads[1].wait()
    loads[2].wait()
    loads[6].wait()
    lax.fori_loop(0, 2, local_states, 0)
    f_in[me] = f_out[me]

    pl.semaphore_wait(barrier, sections - 1 + len(near) + len(far))
    spread(lambda peer: f_out.at[peer], f_in, 0)
    pending.append(all_but_one(f_in, 0))

    loads[3].wait()

    def pairs(h, body):
        for at in range(blocks):
            for past in range(at + 1):
                body(h, at, past)

    def forward_pair(h, at, past):
        ti, si = pl.ds(at * block, block), pl.ds(past * block, block)
        offset = (
            lax.broadcasted_iota(jnp.int32, (block, block), 0)
            - lax.broadcasted_iota(jnp.int32, (block, block), 1)
            + (at - past) * block
        )
        here = seg[at * block : (at + 1) * block]
        keep = wide(here, here) == seg_row[:, past * block : (past + 1) * block]
        if at == past:
            keep = keep & (offset >= 0)
        weights = jnp.where(
            keep, jnp.exp(decay_ref[h] * jnp.maximum(offset, 0).astype(f32)), 0.0
        )
        mask[h, ti, si] = weights
        hi, lo = split(weights * nt(q_ref[ti, head_slice(h)], k_ref[si, head_slice(h)]))
        s_hi[h, ti, si] = hi
        s_lo[h, ti, si] = lo
        values = v_ref[si, head_slice(h)]
        term = nn(hi, values) + nn(lo, values)
        if past == 0:
            o[ti, head_slice(h)] = term
        else:
            o[ti, head_slice(h)] += term

    rate = jnp.where(me < half, decay_ref[0], decay_ref[1])
    total = jnp.exp(jnp.full((depth, 128), rate * rows, f32))
    f_all, state_all = all_but_one(f_in, 0), all_but_one(state, 2)

    def forward_head(h, _):
        pairs(h, forward_pair)

        @pl.when(h == 0)
        def _():
            f_all.wait_recv()
            held = jnp.zeros((depth, 128), f32)
            for at in range(sections):
                p_out[at] = held
                held = total * f_in[at, depth : depth + 1] * held + f_in[at, 0:depth]
            spread(lambda peer: p_out.at[peer], state, 2)

        return 0

    lax.fori_loop(0, 2, forward_head, 0)
    pending.append(state_all)
    state[me] = p_out[me]
    state_all.wait_recv()

    def state_of(buffer, h):
        return split(buffer[pl.ds(h * half, half)].reshape(128, 128))

    def finish_outputs(h, _):
        hi, lo = state_of(state, h)
        both = nn(q_ref[:, head_slice(h)], wide(hi, lo))
        o[:, head_slice(h)] += pre[h] * (both[:, 0:128] + both[:, 128:256])
        return 0

    lax.fori_loop(0, 2, finish_outputs, 0)
    loads[4].wait()
    loads[5].wait()
    outputs = o[...]
    upstream = g_ref[...].astype(f32)
    grad_norm = upstream * gain_ref[...].astype(f32)[None, :]
    squares = outputs * outputs
    mixes = grad_norm * outputs
    pair_out[0:1] = jnp.sum(jnp.transpose(squares[:, 0:128] + squares[:, 128:256]), 0, keepdims=True)
    pair_out[1:2] = jnp.sum(jnp.transpose(mixes[:, 0:128] + mixes[:, 128:256]), 0, keepdims=True)
    def exchange(source, target, which, offsets):
        for at, (z, x) in enumerate(offsets):
            to_column(source, target.at[at], which, line_peer(z, x)).start()
        part = target.at[pl.ds(0, len(offsets))]
        whole = to_column(part, part, which, line_peer(*offsets[0]))
        pending.append(whole)
        return whole

    near_all = exchange(pair_out, near_in, 3, near)

    def turn_queries(h, _):
        hi, lo = split(jnp.transpose(pre[h] * q_ref[:, head_slice(h)].astype(f32)))
        turned[h, 0:128] = hi
        turned[h, 128:256] = lo
        return 0

    lax.fori_loop(0, 2, turn_queries, 0)
    near_all.wait_recv()
    sums = pair_out[...]
    for at in range(len(near)):
        sums = sums + near_in[at]
    if far:
        line_out[...] = sums
        exchange(line_out, far_in, 4, [(z, 0) for z in far]).wait_recv()
        for at in range(len(far)):
            sums = sums + far_in[at]
    scale = lax.rsqrt(sums[0:1] / features + epsilon)
    mixed = scale * sums[1:2] / features
    scale = column(scale)
    mixed = column(mixed)
    scale = wide(scale, scale)
    normed = outputs * scale
    grad_out = scale * (grad_norm - normed * wide(mixed, mixed))
    hi, lo = split(grad_out)
    d_hi[...] = hi
    d_lo[...] = lo
    gains = jnp.sum(upstream * normed, 0, keepdims=True)
    gain_out[0:1] = gains[:, 0:128]
    gain_out[1:2] = gains[:, 128:256]

    def backward_states(h, _):
        four = nn(turned[h], wide(d_hi[:, head_slice(h)], d_lo[:, head_slice(h)]))
        top = four[0:128] + four[128:256]
        b_out[pl.ds(h * half, half)] = (top[:, 0:128] + top[:, 128:256]).reshape(half, depth, 128)
        return 0

    lax.fori_loop(0, 2, backward_states, 0)
    b_in[me] = b_out[me]
    gain_in[me] = gain_out[...]
    spread(lambda peer: b_out.at[peer], b_in, 5)
    pending.append(all_but_one(b_in, 5))

    def start_query(h, _):
        hi, lo = state_of(state, h)
        stack = jnp.concatenate([wide(hi, hi), wide(lo, lo)], axis=0)
        both = nt(wide(d_hi[:, head_slice(h)], d_lo[:, head_slice(h)]), stack)
        gq_ref[:, head_slice(h)] = pre[h] * (both[:, 0:128] + both[:, 128:256])
        return 0

    lax.fori_loop(0, 2, start_query, 0)

    def backward_pair(h, at, past):
        ti, si = pl.ds(at * block, block), pl.ds(past * block, block)
        grads = wide(d_hi[ti, head_slice(h)], d_lo[ti, head_slice(h)])
        values = v_ref[si, head_slice(h)]
        hi, lo = split(mask[h, ti, si] * nt(grads, wide(values, values)))
        keys = k_ref[si, head_slice(h)]
        queries = q_ref[ti, head_slice(h)]
        gq_ref[ti, head_slice(h)] += nn(hi, keys) + nn(lo, keys)
        key_term = tn(hi, queries) + tn(lo, queries)
        both = tn(s_hi[h, ti, si], grads) + tn(s_lo[h, ti, si], grads)
        value_term = both[:, 0:128] + both[:, 128:256]
        if at == past:
            gk_ref[si, head_slice(h)] = key_term
            gv_ref[si, head_slice(h)] = value_term
        else:
            gk_ref[si, head_slice(h)] += key_term
            gv_ref[si, head_slice(h)] += value_term

    b_all, carry_all = all_but_one(b_in, 5), all_but_one(carry, 7)

    def backward_head(h, _):
        pairs(h, backward_pair)
        gq_out[:, head_slice(h)] = gq_ref[:, head_slice(h)].astype(bf16)

        @pl.when(h == 0)
        def _():
            b_all.wait_recv()
            held = jnp.zeros((depth, 128), f32)
            for at in reversed(range(sections)):
                c_out[at] = held
                held = total * f_in[at, depth : depth + 1] * held + b_in[at]
            spread(lambda peer: c_out.at[peer], carry, 7)
            spread(lambda peer: gain_out, gain_in, 6)

        return 0

    lax.fori_loop(0, 2, backward_head, 0)
    pending.append(carry_all)
    pending.append(all_but_one(gain_in, 6))
    carry[me] = c_out[me]
    carry_all.wait_recv()

    carry_out[...] = carry[...]
    all_but_one(gain_in, 6).wait_recv()
    gains = gain_in[0]
    for at in range(1, sections):
        gains = gains + gain_in[at]
    gg_ref[...] = gains / math.sqrt(rows * sections)
    for copy in pending:
        copy.wait_send()


def store_kernel(
    gq_ref, gk_ref, gv_ref, gg_ref, carry, suf, k_ref, v_ref,
    gq_hbm, gk_hbm, gv_hbm, gain_ref, gk_cast, gv_cast, sems,
):
    half = carry.shape[0] // 2
    first = pltpu.make_async_copy(gq_ref, gq_hbm, sems.at[0])
    first.start()
    heads = [slice(h * 128, h * 128 + 128) for h in range(2)]
    states = [split(carry[h * half : h * half + half].reshape(128, 128)) for h in range(2)]
    for h in range(2):
        both = nt(v_ref[:, heads[h]], jnp.concatenate(states[h], axis=0))
        grads = gk_ref[:, heads[h]] + suf[h] * (both[:, 0:128] + both[:, 128:256])
        gk_cast[:, heads[h]] = grads.astype(bf16)
    second = pltpu.make_async_copy(gk_cast, gk_hbm, sems.at[1])
    second.start()
    for h in range(2):
        both = nn(k_ref[:, heads[h]], wide(*states[h]))
        grads = gv_ref[:, heads[h]] + suf[h] * (both[:, 0:128] + both[:, 128:256])
        gv_cast[:, heads[h]] = grads.astype(bf16)
    third = pltpu.make_async_copy(gv_cast, gv_hbm, sems.at[2])
    third.start()
    gain_ref[pl.ds(0, 128)] = gg_ref[0]
    gain_ref[pl.ds(128, 128)] = gg_ref[1]
    first.wait()
    second.wait()
    third.wait()


def shards(queries, key_input, values_in, cotangent, norm_gain, decay_log, doc_starts):
    rows, width = queries.shape
    sections = lax.axis_size("section")
    columns = lax.axis_size("dp")
    depth = width // sections
    tiers = columns // 2
    vmem = pl.BlockSpec(memory_space=pltpu.VMEM)
    hbm = pl.BlockSpec(memory_space=pltpu.HBM)
    sums = pltpu.VMEM((rows, width), f32)
    pieces = pltpu.VMEM((sections, depth, 128), f32)
    flagged = pltpu.VMEM((sections, depth + 1, 128), f32)
    tokens = pltpu.VMEM((rows, width), bf16)
    outs = pl.pallas_call(
        functools.partial(kernel, sections, columns, rows, 256),
        out_shape=[
            jax.ShapeDtypeStruct((rows, width), bf16),
            jax.ShapeDtypeStruct((rows, width), f32),
            jax.ShapeDtypeStruct((rows, width), f32),
            jax.ShapeDtypeStruct((2, 128), f32),
            jax.ShapeDtypeStruct((sections, depth, 128), f32),
            jax.ShapeDtypeStruct((2, rows, 128), f32),
            jax.ShapeDtypeStruct((rows, width), bf16),
            jax.ShapeDtypeStruct((rows, width), bf16),
        ],
        in_specs=[hbm] * 7,
        out_specs=[vmem] * 8,
        scratch_shapes=[
            sums, pltpu.SMEM((2,), f32),
            tokens, tokens,
            pltpu.VMEM((width,), bf16), pltpu.VMEM((rows,), jnp.int32),
            pltpu.SemaphoreType.DMA((7,)),
            flagged, flagged, pieces, pieces,
            pieces, pieces, pieces, pieces,
            pltpu.VMEM((2, 128), f32), pltpu.VMEM((sections, 2, 128), f32),
            pltpu.VMEM((2, rows), f32), pltpu.VMEM((5, 2, rows), f32),
            pltpu.VMEM((2, rows), f32), pltpu.VMEM((tiers, 2, rows), f32),
            pltpu.VMEM((2, 256, rows), bf16),
            pltpu.VMEM((2, rows, 128), f32),
            pltpu.VMEM((2, rows, rows), f32),
            pltpu.VMEM((2, rows, rows), bf16), pltpu.VMEM((2, rows, rows), bf16),
            pltpu.VMEM((rows, width), f32),
            tokens, tokens,
            pltpu.SemaphoreType.DMA((8,)), pltpu.SemaphoreType.DMA((8,)),
        ],
        compiler_params=pltpu.CompilerParams(
            collective_id=0, has_side_effects=True, vmem_limit_bytes=48 * 1024 * 1024
        ),
        name="layer_grads",
    )(
        *(
            pltpu.with_memory_space_constraint(x, pltpu.HBM)
            for x in (
                queries, key_input, values_in, cotangent, norm_gain, decay_log, doc_starts,
            )
        )
    )
    return tuple(
        pl.pallas_call(
            store_kernel,
            out_shape=[jax.ShapeDtypeStruct((rows, width), bf16)] * 3
            + [jax.ShapeDtypeStruct((width,), f32)],
            in_specs=[vmem] * 8,
            out_specs=[hbm] * 3 + [vmem],
            scratch_shapes=[tokens, tokens, pltpu.SemaphoreType.DMA((3,))],
            compiler_params=pltpu.CompilerParams(vmem_limit_bytes=8 * 1024 * 1024),
            name="store_grads",
        )(*outs)
    )


def solution(mesh):
    in_specs = (
        P("section", "dp"),
        P("section", "dp"),
        P("section", "dp"),
        P("section", "dp"),
        P("dp"),
        P("dp"),
        P("section"),
    )
    out_specs = (P("section", "dp"), P("section", "dp"), P("section", "dp"), P("dp"))
    return jax.shard_map(shards, mesh=mesh, in_specs=in_specs, out_specs=out_specs, check_vma=False)
```

```python
import functools
import math

import jax
import jax.numpy as jnp
from jax import lax
from jax.experimental import pallas as pl
from jax.experimental.pallas import tpu as pltpu
from jax.sharding import PartitionSpec as P

epsilon = 1e-05
MESH = pl.DeviceIdType.MESH
f32 = jnp.float32
bf16 = jnp.bfloat16


def split(x):
    hi = x.astype(bf16)
    return hi, (x - hi.astype(f32)).astype(bf16)


def nn(a, b):
    return lax.dot_general(a, b, (((1,), (0,)), ((), ())), preferred_element_type=f32)


def nt(a, b):
    return lax.dot_general(a, b, (((1,), (1,)), ((), ())), preferred_element_type=f32)


def tn(a, b):
    return lax.dot_general(a, b, (((0,), (0,)), ((), ())), preferred_element_type=f32)


def wide(*parts):
    return jnp.concatenate(parts, axis=1)


def column(row):
    return jnp.transpose(jnp.broadcast_to(row, (128, row.shape[1])))


def kernel(
    sections, columns, rows, block,
    q_hbm, k_hbm, v_hbm, g_hbm, gain_hbm, decay_hbm, doc_hbm,
    gq_out, gk_out, gv_out, gg_ref,
    gq_ref, gk_ref, gv_ref, decay_ref,
    q_ref, k_ref, v_ref, g_ref, gain_ref, doc_ref, local_sem,
    f_out, f_in, p_out, state,
    b_out, b_in, c_out, carry,
    gain_out, gain_in,
    pair_out, line_in, turned, ready,
    pre, suf, mask, s_hi, s_lo, o, d_hi, d_lo,
    send_sem, recv_sem,
):
    me = lax.axis_index("section")
    dp = lax.axis_index("dp")
    tiers = columns // 2
    x_at = dp % 2
    z_at = dp // 2
    half = sections // 2
    depth = 256 // sections
    features = 256 * columns
    blocks = rows // block
    pending = []

    def to_section(source, target, which, peer):
        return pltpu.make_async_remote_copy(
            src_ref=source, dst_ref=target, send_sem=send_sem.at[which],
            recv_sem=recv_sem.at[which], device_id={"section": peer}, device_id_type=MESH,
        )

    def to_column(source, target, which, peer):
        return pltpu.make_async_remote_copy(
            src_ref=source, dst_ref=target, send_sem=send_sem.at[which],
            recv_sem=recv_sem.at[which], device_id={"dp": peer}, device_id_type=MESH,
        )

    tall = sections // 4
    hops = sorted(range(tall), key=lambda y: -min(y, tall - y))
    steps = [
        (x, y, c) for y in hops for x in (1, 0) for c in (1, 0) if (x, y, c) != (0, 0, 0)
    ]

    def peer_at(x, y, c):
        return (
            ((me // (2 * tall) + x) % 2) * (2 * tall)
            + ((me // 2 + y) % tall) * 2
            + (me + c) % 2
        )

    def spread(source_of, target, which):
        for step in steps:
            peer = peer_at(*step)
            to_section(source_of(peer), target.at[me], which, peer).start()

    def all_but_one(buffer, which):
        part = buffer.at[pl.ds(0, sections - 1)]
        return to_section(part, part, which, (me + 1) % sections)

    barrier = pltpu.get_barrier_semaphore()
    other = z_at * 2 + (1 - x_at)
    line_hops = sorted(range(1, tiers), key=lambda z: -min(z, tiers - z))

    def line_peer(hop):
        return ((z_at + hop) % tiers) * 2 + x_at

    def greet(peer):
        pl.semaphore_signal(barrier, inc=1, device_id=peer, device_id_type=MESH)

    for hop in line_hops:
        greet({"dp": line_peer(hop)})
    for step in steps:
        greet({"section": peer_at(*step)})
    greet({"dp": other})

    loads = []
    for at, (source, target) in enumerate(
        [
            (doc_hbm, doc_ref), (k_hbm, k_ref), (v_hbm, v_ref),
            (q_hbm, q_ref), (g_hbm, g_ref), (gain_hbm, gain_ref), (decay_hbm, decay_ref),
        ]
    ):
        load = pltpu.make_async_copy(source, target, local_sem.at[at])
        load.start()
        loads.append(load)

    loads[0].wait()
    upper = (
        lax.broadcasted_iota(jnp.int32, (128, 128), 0)
        <= lax.broadcasted_iota(jnp.int32, (128, 128), 1)
    ).astype(f32).astype(bf16)
    run = jnp.zeros((8, 1), f32)
    parts = []
    for at in range(rows // 128):
        docs = doc_ref[pl.ds(at * 128, 128)].astype(f32)
        part = nn(jnp.broadcast_to(docs[None, :], (8, 128)).astype(bf16), upper) + run
        run = part[:, 127:128]
        parts.append(part)
    seg_row = wide(*parts)[0:1]
    last = run[0:1]
    seg = column(seg_row)
    position = lax.broadcasted_iota(jnp.int32, (rows, 128), 0).astype(f32) + 1.0

    def head_slice(h):
        return pl.ds(pl.multiple_of(h * 128, 128), 128)

    def local_states(h, _):
        decay = decay_ref[h]
        suffix = jnp.where(seg == last, jnp.exp(decay * (rows - position)), 0.0)
        prefix = jnp.where(seg == 0.0, jnp.exp(decay * position), 0.0)
        suf[h] = suffix
        pre[h] = prefix
        hi, lo = split(suffix * k_ref[:, head_slice(h)].astype(f32))
        both = tn(wide(hi, lo), v_ref[:, head_slice(h)])
        f_out[pl.ds(h * half, half), 0:depth] = (both[0:128] + both[128:256]).reshape(half, depth, 128)
        return 0

    f_out[:, depth : depth + 1] = jnp.broadcast_to(
        jnp.where(last == 0.0, 1.0, 0.0)[None], (sections, 1, 128)
    )
    loads[1].wait()
    loads[2].wait()
    loads[6].wait()
    lax.fori_loop(0, 2, local_states, 0)
    f_in[me] = f_out[me]

    pl.semaphore_wait(barrier, sections + tiers - 1)
    pl.semaphore_signal(ready, inc=1, device_id={"dp": other}, device_id_type=MESH)
    spread(lambda peer: f_out.at[peer], f_in, 0)
    pending.append(all_but_one(f_in, 0))

    loads[3].wait()

    def pairs(h, body):
        for at in range(blocks):
            for past in range(at + 1):
                body(h, at, past)

    def forward_pair(h, at, past):
        ti, si = pl.ds(at * block, block), pl.ds(past * block, block)
        offset = (
            lax.broadcasted_iota(jnp.int32, (block, block), 0)
            - lax.broadcasted_iota(jnp.int32, (block, block), 1)
            + (at - past) * block
        )
        here = seg[at * block : (at + 1) * block]
        keep = wide(here, here) == seg_row[:, past * block : (past + 1) * block]
        if at == past:
            keep = keep & (offset >= 0)
        weights = jnp.where(
            keep, jnp.exp(decay_ref[h] * jnp.maximum(offset, 0).astype(f32)), 0.0
        )
        mask[h, ti, si] = weights
        hi, lo = split(weights * nt(q_ref[ti, head_slice(h)], k_ref[si, head_slice(h)]))
        s_hi[h, ti, si] = hi
        s_lo[h, ti, si] = lo
        values = v_ref[si, head_slice(h)]
        term = nn(hi, values) + nn(lo, values)
        if past == 0:
            o[ti, head_slice(h)] = term
        else:
            o[ti, head_slice(h)] += term

    rate = jnp.where(me < half, decay_ref[0], decay_ref[1])
    total = jnp.exp(jnp.full((depth, 128), rate * rows, f32))
    f_all, state_all = all_but_one(f_in, 0), all_but_one(state, 2)

    def forward_head(h, _):
        pairs(h, forward_pair)

        @pl.when(h == 0)
        def _():
            f_all.wait_recv()
            held = jnp.zeros((depth, 128), f32)
            for at in range(sections):
                p_out[at] = held
                held = total * f_in[at, depth : depth + 1] * held + f_in[at, 0:depth]
            spread(lambda peer: p_out.at[peer], state, 2)

        return 0

    lax.fori_loop(0, 2, forward_head, 0)
    pending.append(state_all)
    state[me] = p_out[me]
    state_all.wait_recv()

    def state_of(buffer, h):
        return split(buffer[pl.ds(h * half, half)].reshape(128, 128))

    def finish_outputs(h, _):
        hi, lo = state_of(state, h)
        both = nn(q_ref[:, head_slice(h)], wide(hi, lo))
        o[:, head_slice(h)] += pre[h] * (both[:, 0:128] + both[:, 128:256])
        return 0

    lax.fori_loop(0, 2, finish_outputs, 0)
    loads[4].wait()
    loads[5].wait()
    outputs = o[...]
    upstream = g_ref[...].astype(f32)
    grad_norm = upstream * gain_ref[...].astype(f32)[None, :]
    squares = outputs * outputs
    mixes = grad_norm * outputs
    pair_out[0:1] = jnp.sum(jnp.transpose(squares[:, 0:128] + squares[:, 128:256]), 0, keepdims=True)
    pair_out[1:2] = jnp.sum(jnp.transpose(mixes[:, 0:128] + mixes[:, 128:256]), 0, keepdims=True)
    offsets = sorted(
        [(z, x) for z in range(tiers) for x in range(2) if (z, x) != (0, 0)],
        key=lambda hop: -(min(hop[0], tiers - hop[0]) + 2 * hop[1]),
    )
    pl.semaphore_wait(ready, 1)
    for at, (z, x) in enumerate(offsets):
        peer = ((z_at + z) % tiers) * 2 + (x_at + x) % 2
        to_column(pair_out, line_in.at[at], 4, peer).start()
    line_all = to_column(line_in, line_in, 4, other)
    pending.append(line_all)

    def turn_queries(h, _):
        hi, lo = split(jnp.transpose(pre[h] * q_ref[:, head_slice(h)].astype(f32)))
        turned[h, 0:128] = hi
        turned[h, 128:256] = lo
        return 0

    lax.fori_loop(0, 2, turn_queries, 0)
    line_all.wait_recv()
    sums = pair_out[...]
    for at in range(len(offsets)):
        sums = sums + line_in[at]
    scale = lax.rsqrt(sums[0:1] / features + epsilon)
    mixed = scale * sums[1:2] / features
    scale = column(scale)
    mixed = column(mixed)
    scale = wide(scale, scale)
    normed = outputs * scale
    grad_out = scale * (grad_norm - normed * wide(mixed, mixed))
    hi, lo = split(grad_out)
    d_hi[...] = hi
    d_lo[...] = lo
    gains = jnp.sum(upstream * normed, 0, keepdims=True)
    gain_out[0:1] = gains[:, 0:128]
    gain_out[1:2] = gains[:, 128:256]

    def backward_states(h, _):
        four = nn(turned[h], wide(d_hi[:, head_slice(h)], d_lo[:, head_slice(h)]))
        top = four[0:128] + four[128:256]
        b_out[pl.ds(h * half, half)] = (top[:, 0:128] + top[:, 128:256]).reshape(half, depth, 128)
        return 0

    lax.fori_loop(0, 2, backward_states, 0)
    b_in[me] = b_out[me]
    gain_in[me] = gain_out[...]
    spread(lambda peer: b_out.at[peer], b_in, 5)
    pending.append(all_but_one(b_in, 5))

    def start_query(h, _):
        hi, lo = state_of(state, h)
        stack = jnp.concatenate([wide(hi, hi), wide(lo, lo)], axis=0)
        both = nt(wide(d_hi[:, head_slice(h)], d_lo[:, head_slice(h)]), stack)
        gq_ref[:, head_slice(h)] = pre[h] * (both[:, 0:128] + both[:, 128:256])
        return 0

    lax.fori_loop(0, 2, start_query, 0)

    def backward_pair(h, at, past):
        ti, si = pl.ds(at * block, block), pl.ds(past * block, block)
        grads = wide(d_hi[ti, head_slice(h)], d_lo[ti, head_slice(h)])
        values = v_ref[si, head_slice(h)]
        hi, lo = split(mask[h, ti, si] * nt(grads, wide(values, values)))
        keys = k_ref[si, head_slice(h)]
        queries = q_ref[ti, head_slice(h)]
        gq_ref[ti, head_slice(h)] += nn(hi, keys) + nn(lo, keys)
        key_term = tn(hi, queries) + tn(lo, queries)
        both = tn(s_hi[h, ti, si], grads) + tn(s_lo[h, ti, si], grads)
        value_term = both[:, 0:128] + both[:, 128:256]
        if at == past:
            gk_ref[si, head_slice(h)] = key_term
            gv_ref[si, head_slice(h)] = value_term
        else:
            gk_ref[si, head_slice(h)] += key_term
            gv_ref[si, head_slice(h)] += value_term

    b_all, carry_all = all_but_one(b_in, 5), all_but_one(carry, 7)

    def backward_head(h, _):
        pairs(h, backward_pair)
        gq_out[:, head_slice(h)] = gq_ref[:, head_slice(h)].astype(bf16)

        @pl.when(h == 0)
        def _():
            b_all.wait_recv()
            held = jnp.zeros((depth, 128), f32)
            for at in reversed(range(sections)):
                c_out[at] = held
                held = total * f_in[at, depth : depth + 1] * held + b_in[at]
            spread(lambda peer: c_out.at[peer], carry, 7)
            spread(lambda peer: gain_out, gain_in, 6)

        return 0

    lax.fori_loop(0, 2, backward_head, 0)
    pending.append(carry_all)
    pending.append(all_but_one(gain_in, 6))
    carry[me] = c_out[me]
    carry_all.wait_recv()

    def finish(h, _):
        hi, lo = state_of(carry, h)
        both = nt(v_ref[:, head_slice(h)], jnp.concatenate([hi, lo], axis=0))
        grads = gk_ref[:, head_slice(h)] + suf[h] * (both[:, 0:128] + both[:, 128:256])
        gk_out[:, head_slice(h)] = grads.astype(bf16)
        both = nn(k_ref[:, head_slice(h)], wide(hi, lo))
        grads = gv_ref[:, head_slice(h)] + suf[h] * (both[:, 0:128] + both[:, 128:256])
        gv_out[:, head_slice(h)] = grads.astype(bf16)
        return 0

    lax.fori_loop(0, 2, finish, 0)
    all_but_one(gain_in, 6).wait_recv()
    gains = gain_in[0]
    for at in range(1, sections):
        gains = gains + gain_in[at]
    gg_ref[...] = gains / math.sqrt(rows * sections)
    for copy in pending:
        copy.wait_send()


def store_kernel(gq_ref, gk_ref, gv_ref, gg_ref, gq_hbm, gk_hbm, gv_hbm, gain_ref, sems):
    copies = []
    for at, (source, target) in enumerate(
        [(gq_ref, gq_hbm), (gk_ref, gk_hbm), (gv_ref, gv_hbm)]
    ):
        copy = pltpu.make_async_copy(source, target, sems.at[at])
        copy.start()
        copies.append(copy)
    gain_ref[pl.ds(0, 128)] = gg_ref[0]
    gain_ref[pl.ds(128, 128)] = gg_ref[1]
    for copy in copies:
        copy.wait()


def shards(queries, key_input, values_in, cotangent, norm_gain, decay_log, doc_starts):
    rows, width = queries.shape
    sections = lax.axis_size("section")
    columns = lax.axis_size("dp")
    depth = width // sections
    tiers = columns // 2
    vmem = pl.BlockSpec(memory_space=pltpu.VMEM)
    hbm = pl.BlockSpec(memory_space=pltpu.HBM)
    sums = pltpu.VMEM((rows, width), f32)
    pieces = pltpu.VMEM((sections, depth, 128), f32)
    flagged = pltpu.VMEM((sections, depth + 1, 128), f32)
    tokens = pltpu.VMEM((rows, width), bf16)
    outs = pl.pallas_call(
        functools.partial(kernel, sections, columns, rows, 256),
        out_shape=[jax.ShapeDtypeStruct((rows, width), bf16)] * 3
        + [jax.ShapeDtypeStruct((2, 128), f32)],
        in_specs=[hbm] * 7,
        out_specs=[vmem] * 4,
        scratch_shapes=[
            sums, sums, sums, pltpu.SMEM((2,), f32),
            tokens, tokens, tokens, tokens,
            pltpu.VMEM((width,), bf16), pltpu.VMEM((rows,), jnp.int32),
            pltpu.SemaphoreType.DMA((7,)),
            flagged, flagged, pieces, pieces,
            pieces, pieces, pieces, pieces,
            pltpu.VMEM((2, 128), f32), pltpu.VMEM((sections, 2, 128), f32),
            pltpu.VMEM((2, rows), f32), pltpu.VMEM((columns - 1, 2, rows), f32),
            pltpu.VMEM((2, 256, rows), bf16), pltpu.SemaphoreType.REGULAR,
            pltpu.VMEM((2, rows, 128), f32), pltpu.VMEM((2, rows, 128), f32),
            pltpu.VMEM((2, rows, rows), f32),
            pltpu.VMEM((2, rows, rows), bf16), pltpu.VMEM((2, rows, rows), bf16),
            pltpu.VMEM((rows, width), f32),
            tokens, tokens,
            pltpu.SemaphoreType.DMA((8,)), pltpu.SemaphoreType.DMA((8,)),
        ],
        compiler_params=pltpu.CompilerParams(
            collective_id=0, has_side_effects=True, vmem_limit_bytes=48 * 1024 * 1024
        ),
        name="layer_grads",
    )(
        *(
            pltpu.with_memory_space_constraint(x, pltpu.HBM)
            for x in (
                queries, key_input, values_in, cotangent, norm_gain, decay_log, doc_starts,
            )
        )
    )
    return tuple(
        pl.pallas_call(
            store_kernel,
            out_shape=[jax.ShapeDtypeStruct((rows, width), bf16)] * 3
            + [jax.ShapeDtypeStruct((width,), f32)],
            in_specs=[vmem] * 4,
            out_specs=[hbm] * 3 + [vmem],
            scratch_shapes=[pltpu.SemaphoreType.DMA((3,))],
            compiler_params=pltpu.CompilerParams(vmem_limit_bytes=8 * 1024 * 1024),
            name="store_grads",
        )(*outs)
    )


def solution(mesh):
    in_specs = (
        P("section", "dp"),
        P("section", "dp"),
        P("section", "dp"),
        P("section", "dp"),
        P("dp"),
        P("dp"),
        P("section"),
    )
    out_specs = (P("section", "dp"), P("section", "dp"), P("section", "dp"), P("dp"))
    return jax.shard_map(shards, mesh=mesh, in_specs=in_specs, out_specs=out_specs, check_vma=False)
```
